512 devices in a mesh: dp: 64 (over z, y), clus: 8 (over x, core).
Axes of the slice: x: 4, y: 4, z: 16, core: 2. Of those that a mesh axis runs over, the one named last changes fastest.
Arguments:
- embeddings: bfloat16 [32768, 4096], P('dp'), may hold values from -6 to 6
- assignment: int32 [32768], P('dp'), may hold values from 0 to 1535
- slot_of: int32 [1536], replicated, may hold values from 0 to 1535, each once
- old_centroids: bfloat16 [1536, 4096], P(('clus', 'dp')), may hold values from -6 to 6
Outputs:
- new_centroids: float32 [1536, 4096], P(('clus', 'dp'))
- distance: float32 [32768], P('dp')
The draws below stay inside these ranges and needn't reach their ends.
All inputs are finite; a program needn't handle non-finite values.
Results may differ from the reference program's by a relative error of at most 0.0003.
Values may be sent and summed in bfloat16 or wider, within the bound.
No kernel may reach another device: no remote copies, remote signals or barrier semaphores. Data moves between devices by JAX's collectives and lax.ppermute only.
A program may use at most 64 MiB of HBM per device.

```python
import math
import jax
import jax.numpy as jnp
import numpy as np
from jax import lax

D = 4096
TOK_DEV = 512
POINTS = 32768
CLUSTERS = 1536
N_DP = 64


def place_ends(values, rng, smallest, top_value):
    longest = values.shape.index(max(values.shape))
    spots = []
    for shift in (0, 1):
        where = [jax.random.randint(jax.random.fold_in(rng, axis), (), 0, length) for axis, length in enumerate(values.shape)]
        where[longest] = (where[longest] + shift) % values.shape[longest]
        spots.append(tuple(where))
    return values.at[spots[0]].set(smallest).at[spots[1]].set(top_value)


def block_scale(own_key, dims, cuts, least, largest):
    def one(dim, parts):
        draws = jax.random.uniform(jax.random.fold_in(jax.random.fold_in(own_key, 6), dim), (parts,), jnp.float32, least / len(cuts), largest / len(cuts))
        return jnp.repeat(jnp.exp(draws), dims[dim] // parts).reshape((-1,) + (1,) * (len(dims) - dim - 1))

    factor_of = one(*cuts[0])
    for cut in cuts[1:]:
        factor_of = factor_of * one(*cut)
    return factor_of


def rank_table(number_of, skew):
    loads = [(1 << 20) // math.isqrt(standing ** skew) + 1 for standing in range(1, number_of + 1)]
    width = 1 + sum(loads) // (1 << 30)
    return np.cumsum(np.array([max(1, weight // width) for weight in loads]))


def ranked(key, dims, number_of, lean):
    listing = rank_table(number_of, lean)
    lot = jax.random.randint(jax.random.fold_in(key, 1), dims, 0, int(listing[number_of - 1]))
    rank = jnp.searchsorted(jnp.asarray(listing, jnp.int32), lot, side="right")
    return jax.random.permutation(jax.random.fold_in(key, 2), number_of)[rank].astype(jnp.int32)


def normal_values(stream_key, extent, width, limit, split=(), dtype=jnp.bfloat16):
    level = block_scale(stream_key, extent, split, -0.22, 0.18) if split else 1.0
    values = jax.random.normal(stream_key, extent, jnp.float32) * width * level
    return jnp.minimum(jnp.maximum(values, -limit), limit).astype(dtype)


def setup_inputs(seed: int = 0) -> dict:
    key_of = jax.random.split(jax.random.key(seed), 5)
    return {
        "embeddings": normal_values(key_of[0], (POINTS, D), 1.0, 6.0, ((0, 64),)),
        "assignment": place_ends(ranked(key_of[1], (POINTS,), CLUSTERS, 2), jax.random.fold_in(key_of[1], 3), 0, CLUSTERS - 1).astype(jnp.int32),
        "slot_of": jax.random.permutation(key_of[2], CLUSTERS).astype(jnp.int32),
        "old_centroids": normal_values(key_of[3], (CLUSTERS, D), 1.0, 6.0, ((0, 512),)),
    }


def reference(embeddings, assignment, slot_of, old_centroids):
    clusters = old_centroids.shape[0]
    slot_ids = slot_of[assignment].astype(jnp.int32)
    points = embeddings.reshape(N_DP, TOK_DEV, D)
    slots = slot_ids.reshape(N_DP, TOK_DEV)
    cent_wide = old_centroids.astype(jnp.float32)
    cent_rms = jnp.sqrt(lax.optimization_barrier(jnp.mean(cent_wide * cent_wide, axis=1)) + 1e-06)

    def step(totals, inputs):
        rows, row_slots = inputs
        rows_wide = rows.astype(jnp.float32)
        totals = totals + jax.ops.segment_sum(rows_wide, row_slots, clusters)
        picked = old_centroids[row_slots].astype(jnp.float32)
        scores = lax.optimization_barrier(jnp.sum(rows_wide * picked, axis=1))
        root_mean = jnp.sqrt(lax.optimization_barrier(jnp.mean(rows_wide * rows_wide, axis=1)) + 1e-06)
        return (totals, 1.0 - scores / (jnp.float32(D) * root_mean * cent_rms[row_slots]))
    sums, distance = lax.scan(step, jnp.zeros((clusters, D), jnp.float32), (points, slots))
    overall = sums + cent_wide
    updated = overall * lax.rsqrt(lax.optimization_barrier(jnp.mean(overall * overall, axis=1, keepdims=True)) + 1e-06)
    return (updated, distance.reshape(-1))
```

```python
import jax
import jax.numpy as jnp
from jax import lax
from jax.experimental import pallas as pl
from jax.experimental.pallas import tpu as pltpu
from jax.sharding import Mesh
from jax.sharding import PartitionSpec as P

D = 4096
ZH, ZL, NY, NC = 8, 2, 4, 8
NZ = ZH * ZL
DP = ("zh", "zl", "y")
CLUS_DP = ("c", "zh", "zl", "y")
EPS = 1e-06


def swap(x, axis, pairs):
    return lax.ppermute(x, axis, pairs)


def shifted(x, axis, size, by):
    return lax.ppermute(x, axis, [(i, (i + by) % size) for i in range(size)])


def exchange(x, axis):
    return lax.all_to_all(x, axis, 0, 0, tiled=True)


def copies(x, count):
    return jnp.broadcast_to(x, (count, *x.shape))


def sums_kernel(pos_ref, own_ref, a_ref, b_ref, c_ref, away_ref, home_ref):
    y = pos_ref[0]
    zl = pos_ref[1]
    rows = home_ref.shape[0]
    points = own_ref.shape[0] - 16
    r = lax.broadcasted_iota(jnp.int32, (rows, 1), 0)
    per_z = NC * 3
    zh = r // per_z
    c = (r % per_z) // 3
    k = r % 3
    slot = c * (NZ * NY * 3) + (zh * ZL * NY + y) * 3 + k
    for out_ref, part in ((away_ref, 1 - zl), (home_ref, zl)):
        wanted = slot + part * (NY * 3)
        total = None
        for ref in (own_ref, a_ref, b_ref, c_ref):
            tail = ref[points : points + 16, :].astype(jnp.float32)
            ids = (tail[0:1, :] * 64.0 + tail[1:2, :]).astype(jnp.int32)
            hot = (wanted == ids).astype(jnp.float32).astype(jnp.bfloat16)
            got = jnp.dot(hot, ref[0:points, :], preferred_element_type=jnp.float32)
            total = got if total is None else total + got
        out_ref[...] = total


def local_sums(pos, own, others):
    rows = ZH * NC * 3
    width = own.shape[1]
    shape = jax.ShapeDtypeStruct((rows, width), jnp.float32)
    vmem = pl.BlockSpec(memory_space=pltpu.VMEM)
    return pl.pallas_call(
        sums_kernel,
        out_shape=(shape, shape),
        in_specs=[pl.BlockSpec(memory_space=pltpu.SMEM)] + [vmem] * 4,
        out_specs=(vmem, vmem),
        name="local_sums",
    )(pos, own, *others)


def score_kernel(ids_ref, root_ref, a_ref, b_ref, c_ref, d_ref, emb_ref, out_ref):
    n = a_ref.shape[0]
    emb = emb_ref[...]
    ids = ids_ref[...]
    total = None
    for j, ref in enumerate((a_ref, b_ref, c_ref, d_ref)):
        rows = ref[...]
        raw = lax.dot_general(
            rows, emb, (((1,), (1,)), ((), ())), preferred_element_type=jnp.float32
        )
        wide = rows.astype(jnp.float32)
        rms = jnp.sqrt(jnp.mean(wide * wide, axis=1, keepdims=True) + EPS)
        here = lax.broadcasted_iota(jnp.int32, (n, 1), 0) + j * n
        got = jnp.sum(jnp.where(here == ids, raw / rms, 0.0), axis=0, keepdims=True)
        total = got if total is None else total + got
    out_ref[...] = total / (jnp.float32(D) * root_ref[...])


def local_scores(ids, root, blocks, emb):
    points = emb.shape[0]
    step = 128
    row = pl.BlockSpec((1, step), lambda i: (0, i))
    whole = pl.BlockSpec(blocks[0].shape, lambda i: (0, 0))
    return pl.pallas_call(
        score_kernel,
        grid=(points // step,),
        out_shape=jax.ShapeDtypeStruct((1, points), jnp.float32),
        in_specs=[row, row] + [whole] * 4 + [pl.BlockSpec((step, D), lambda i: (i, 0))],
        out_specs=row,
        name="local_scores",
    )(ids, root, *blocks, emb)


def per_device(embeddings, assignment, slot_of, old_centroids):
    points = embeddings.shape[0]
    clusters = slot_of.shape[0]
    width = D // NC
    c = lax.axis_index("c")
    y = lax.axis_index("y")
    zl = lax.axis_index("zl")

    cent = copies(old_centroids.reshape(96, 128), NZ)
    cent = exchange(cent, ("zh", "zl"))

    matches = assignment[:, None] == jnp.arange(clusters, dtype=jnp.int32)[None, :]
    slot_ids = jnp.sum(jnp.where(matches, slot_of[None, :], 0), axis=1)
    digits = jnp.stack([slot_ids // 64, slot_ids % 64]).astype(jnp.bfloat16)
    mine = lax.dynamic_slice_in_dim(embeddings, c * width, width, 1)
    packed = jnp.concatenate([mine, digits, jnp.zeros((14, width), jnp.bfloat16)], axis=0)
    others = [shifted(packed, "y", NY, d) for d in (2, 1, -1)]

    pos = jnp.stack([y, zl]).astype(jnp.int32)
    away, home = local_sums(pos, packed, others)
    arrived = shifted(away, "zl", ZL, 1)
    both = (home + arrived).reshape(ZH, NC * 3, width)

    blocks = cent.reshape(NZ * 3, D)
    others = [shifted(blocks, "y", NY, d) for d in (2, 1, -1)]
    local = slot_ids - c * (NZ * NY * 3)
    owner = local // 3
    turn = (y - owner % NY) % NY
    place = jnp.where(turn == 0, 0, jnp.where(turn == 2, 1, jnp.where(turn == 1, 2, 3)))
    row_ids = place * (NZ * 3) + (owner // NY) * 3 + local % 3
    row_ids = jnp.where((local >= 0) & (local < NZ * NY * 3), row_ids, -1)
    widened = embeddings.astype(jnp.float32)
    root_mean = jnp.sqrt(jnp.mean(widened * widened, axis=1) + EPS)
    partial = local_scores(row_ids[None, :], root_mean[None, :], [blocks, *others], embeddings)

    summed = exchange(both, "zh").sum(axis=0)
    sends = jnp.concatenate(
        [summed.reshape(NC, 1, 3 * width), jnp.broadcast_to(partial[None], (NC, 1, points))], axis=2
    )
    got = exchange(sends, "c")[:, 0]
    distance = 1.0 - got[:, 3 * width :].sum(axis=0)
    own_sums = got[:, : 3 * width].reshape(NC, 3, width).swapaxes(0, 1).reshape(3, D)
    overall = own_sums + old_centroids.astype(jnp.float32)
    updated = overall * lax.rsqrt(jnp.mean(overall * overall, axis=1, keepdims=True) + EPS)
    return (updated, distance)


def solution(mesh):
    split = Mesh(mesh.devices.reshape(ZH, ZL, NY, NC), ("zh", "zl", "y", "c"))
    return jax.shard_map(
        per_device,
        mesh=split,
        in_specs=(P(DP, None), P(DP), P(), P(CLUS_DP, None)),
        out_specs=(P(CLUS_DP, None), P(DP)),
        check_vma=False,
    )
```

```python
import jax
import jax.numpy as jnp
from jax import lax
from jax.experimental import pallas as pl
from jax.experimental.pallas import tpu as pltpu
from jax.sharding import Mesh
from jax.sharding import PartitionSpec as P


D = 4096
ZH, ZL, NY, NC = 8, 2, 4, 8
NZ = ZH * ZL
DP = ("zh", "zl", "y")
CLUS_DP = ("c", "zh", "zl", "y")
EPS = 1e-06


def shifted(x, axis, size, by):
    return lax.ppermute(x, axis, [(i, (i + by) % size) for i in range(size)])


def exchange(x, axis):
    return lax.all_to_all(x, axis, 0, 0, tiled=True)


def copies(x, count):
    return jnp.broadcast_to(x, (count, *x.shape))


def sums_kernel(pos_ref, own_ref, a_ref, b_ref, c_ref, out_ref):
    rows = out_ref.shape[0]
    points = own_ref.shape[0] - 16
    r = lax.broadcasted_iota(jnp.int32, (rows, 1), 0)
    per_z = NC * 3
    zh = r // per_z
    c = (r % per_z) // 3
    slot = c * (NZ * NY * 3) + zh * (ZL * NY * 3) + r % 3
    wanted = slot + pos_ref[0]
    total = None
    for ref in (own_ref, a_ref, b_ref, c_ref):
        tail = ref[points : points + 16, :].astype(jnp.float32)
        ids = (tail[0:1, :] * 64.0 + tail[1:2, :]).astype(jnp.int32)
        hot = (wanted == ids).astype(jnp.float32).astype(jnp.bfloat16)
        got = jnp.dot(hot, ref[0:points, :], preferred_element_type=jnp.float32)
        total = got if total is None else total + got
    out_ref[...] = total


def local_sums(first, own, others):
    rows = ZH * NC * 3
    width = own.shape[1]
    vmem = pl.BlockSpec(memory_space=pltpu.VMEM)
    return pl.pallas_call(
        sums_kernel,
        out_shape=jax.ShapeDtypeStruct((rows, width), jnp.float32),
        in_specs=[pl.BlockSpec(memory_space=pltpu.SMEM)] + [vmem] * 4,
        out_specs=vmem,
        name="local_sums",
    )(first.reshape(1), own, *others)


def score_kernel(ids_ref, root_ref, a_ref, b_ref, c_ref, d_ref, emb_ref, out_ref, inv_ref):
    n = a_ref.shape[0]
    blocks = (a_ref, b_ref, c_ref, d_ref)

    @pl.when(pl.program_id(0) == 0)
    def _():
        for j, ref in enumerate(blocks):
            wide = ref[...].astype(jnp.float32)
            rms = jnp.sqrt(jnp.mean(wide * wide, axis=1, keepdims=True) + EPS)
            inv_ref[j * n : (j + 1) * n, :] = jnp.broadcast_to(1.0 / rms, (n, inv_ref.shape[1]))

    emb = emb_ref[...]
    ids = ids_ref[...]
    total = None
    for j, ref in enumerate(blocks):
        raw = lax.dot_general(
            ref[...], emb, (((1,), (1,)), ((), ())), preferred_element_type=jnp.float32
        )
        here = lax.broadcasted_iota(jnp.int32, raw.shape, 0) + j * n
        scaled = raw * inv_ref[j * n : (j + 1) * n, :]
        got = jnp.sum(jnp.where(here == ids, scaled, 0.0), axis=0, keepdims=True)
        total = got if total is None else total + got
    out_ref[...] = total / (jnp.float32(D) * root_ref[...])


def local_scores(ids, root, blocks, emb):
    points = emb.shape[0]
    step = 128
    row = pl.BlockSpec((1, step), lambda i: (0, i))
    whole = pl.BlockSpec(blocks[0].shape, lambda i: (0, 0))
    return pl.pallas_call(
        score_kernel,
        grid=(points // step,),
        out_shape=jax.ShapeDtypeStruct((1, points), jnp.float32),
        in_specs=[row, row] + [whole] * 4 + [pl.BlockSpec((step, D), lambda i: (i, 0))],
        out_specs=row,
        scratch_shapes=[pltpu.VMEM((4 * blocks[0].shape[0], step), jnp.float32)],
        name="local_scores",
    )(ids, root, *blocks, emb)


def steps(embeddings, assignment, slot_of, old_centroids):
    points = embeddings.shape[0]
    clusters = slot_of.shape[0]
    width = D // NC
    c = lax.axis_index("c")
    y = lax.axis_index("y")
    zl = lax.axis_index("zl")

    matches = assignment[:, None] == jnp.arange(clusters, dtype=jnp.int32)[None, :]
    slot_ids = jnp.sum(jnp.where(matches, slot_of[None, :], 0), axis=1)
    digits = jnp.stack([slot_ids // 64, slot_ids % 64]).astype(jnp.bfloat16)
    mine = lax.dynamic_slice_in_dim(embeddings, c * width, width, 1)
    packed = jnp.concatenate([mine, digits, jnp.zeros((14, width), jnp.bfloat16)], axis=0)
    others = [shifted(packed, "y", NY, d) for d in (2, 1, -1)]

    cent = copies(old_centroids.reshape(96, 128), NZ)
    cent = exchange(cent, ("zh", "zl"))

    widened = embeddings.astype(jnp.float32)
    root_mean = jnp.sqrt(jnp.mean(widened * widened, axis=1) + EPS)

    away = local_sums(y * 3 + (1 - zl) * (NY * 3), packed, others)
    arrived = shifted(away, "zl", ZL, 1)
    home = local_sums(y * 3 + zl * (NY * 3), packed, others)
    both = (home + arrived).reshape(ZH, NC * 3, width)
    summed = exchange(both, "zh")
    summed = summed.sum(axis=0)

    blocks = cent.reshape(NZ * 3, D)
    others = [shifted(blocks, "y", NY, d) for d in (2, 1, -1)]
    local = slot_ids - c * (NZ * NY * 3)
    owner = local // 3
    turn = (y - owner % NY) % NY
    place = jnp.where(turn == 0, 0, jnp.where(turn == 2, 1, jnp.where(turn == 1, 2, 3)))
    row_ids = place * (NZ * 3) + (owner // NY) * 3 + local % 3
    row_ids = jnp.where((local >= 0) & (local < NZ * NY * 3), row_ids, -1)
    partial = local_scores(row_ids[None, :], root_mean[None, :], [blocks, *others], embeddings)

    sends = jnp.concatenate(
        [summed.reshape(NC, 1, 3 * width), jnp.broadcast_to(partial[None], (NC, 1, points))], axis=2
    )
    got = exchange(sends, "c")[:, 0]
    distance = 1.0 - got[:, 3 * width :].sum(axis=0)
    own_sums = got[:, : 3 * width].reshape(NC, 3, width).swapaxes(0, 1).reshape(3, D)
    overall = own_sums + old_centroids.astype(jnp.float32)
    updated = overall * lax.rsqrt(jnp.mean(overall * overall, axis=1, keepdims=True) + EPS)
    return (updated, distance)


def solution(mesh):
    split = Mesh(mesh.devices.reshape(ZH, ZL, NY, NC), ("zh", "zl", "y", "c"))
    return jax.shard_map(
        steps,
        mesh=split,
        in_specs=(P(DP, None), P(DP), P(), P(CLUS_DP, None)),
        out_specs=(P(CLUS_DP, None), P(DP)),
        check_vma=False,
    )
```

```python
import jax
import jax.numpy as jnp
from jax import lax
from jax.experimental import pallas as pl
from jax.experimental.pallas import tpu as pltpu
from jax.sharding import Mesh
from jax.sharding import PartitionSpec as P


D = 4096
ZH, ZL, NY, NC = 8, 2, 4, 8
NZ = ZH * ZL
DP = ("zh", "zl", "y")
CLUS_DP = ("c", "zh", "zl", "y")
EPS = 1e-06


def shifted(x, axis, size, by):
    return lax.ppermute(x, axis, [(i, (i + by) % size) for i in range(size)])


def exchange(x, axis):
    return lax.all_to_all(x, axis, 0, 0, tiled=True)


def copies(x, count):
    return jnp.broadcast_to(x, (count, *x.shape))


def sums_kernel(pos_ref, own_ref, a_ref, b_ref, c_ref, out_ref):
    rows = out_ref.shape[0]
    points = own_ref.shape[0] - 16
    r = lax.broadcasted_iota(jnp.int32, (rows, 1), 0)
    per_z = NC * 3
    zh = r // per_z
    c = (r % per_z) // 3
    slot = c * (NZ * NY * 3) + zh * (ZL * NY * 3) + r % 3
    wanted = slot + pos_ref[0]
    total = None
    for ref in (own_ref, a_ref, b_ref, c_ref):
        tail = ref[points : points + 16, :].astype(jnp.float32)
        ids = (tail[0:1, :] * 64.0 + tail[1:2, :]).astype(jnp.int32)
        hot = (wanted == ids).astype(jnp.float32).astype(jnp.bfloat16)
        got = jnp.dot(hot, ref[0:points, :], preferred_element_type=jnp.float32)
        total = got if total is None else total + got
    out_ref[...] = total


def local_sums(first, own, others):
    rows = ZH * NC * 3
    width = own.shape[1]
    vmem = pl.BlockSpec(memory_space=pltpu.VMEM)
    return pl.pallas_call(
        sums_kernel,
        out_shape=jax.ShapeDtypeStruct((rows, width), jnp.float32),
        in_specs=[pl.BlockSpec(memory_space=pltpu.SMEM)] + [vmem] * 4,
        out_specs=vmem,
        name="local_sums",
    )(first.reshape(1), own, *others)


def score_kernel(
    ids_ref, root_ref, a_ref, b_ref, c_ref, d_ref, emb_ref, out_ref, rows_ref, inv_ref
):
    n = a_ref.shape[0]

    @pl.when(pl.program_id(0) == 0)
    def _():
        for j, ref in enumerate((a_ref, b_ref, c_ref, d_ref)):
            rows = ref[...]
            rows_ref[j * n : (j + 1) * n, :] = rows
            wide = rows.astype(jnp.float32)
            rms = jnp.sqrt(jnp.mean(wide * wide, axis=1, keepdims=True) + EPS)
            inv_ref[j * n : (j + 1) * n, :] = jnp.broadcast_to(1.0 / rms, (n, inv_ref.shape[1]))

    raw = lax.dot_general(
        rows_ref[...], emb_ref[...], (((1,), (1,)), ((), ())), preferred_element_type=jnp.float32
    )
    here = lax.broadcasted_iota(jnp.int32, raw.shape, 0)
    picked = jnp.where(here == ids_ref[...], raw * inv_ref[...], 0.0)
    total = jnp.sum(picked, axis=0, keepdims=True) / (jnp.float32(D) * root_ref[...])
    out_ref[...] = jnp.broadcast_to(total, out_ref.shape)


def local_scores(ids, root, blocks, emb):
    points = emb.shape[0]
    step = 256
    row = pl.BlockSpec((1, step), lambda i: (0, i))
    whole = pl.BlockSpec(blocks[0].shape, lambda i: (0, 0))
    return pl.pallas_call(
        score_kernel,
        grid=(points // step,),
        out_shape=jax.ShapeDtypeStruct((NC, points), jnp.float32),
        in_specs=[row, row] + [whole] * 4 + [pl.BlockSpec((step, D), lambda i: (i, 0))],
        out_specs=pl.BlockSpec((NC, step), lambda i: (0, i)),
        scratch_shapes=[
            pltpu.VMEM((4 * blocks[0].shape[0], D), jnp.bfloat16),
            pltpu.VMEM((4 * blocks[0].shape[0], step), jnp.float32),
        ],
        name="local_scores",
    )(ids, root, *blocks, emb)


def steps(embeddings, assignment, slot_of, old_centroids):
    clusters = slot_of.shape[0]
    width = D // NC
    c = lax.axis_index("c")
    y = lax.axis_index("y")
    zl = lax.axis_index("zl")

    matches = assignment[:, None] == jnp.arange(clusters, dtype=jnp.int32)[None, :]
    slot_ids = jnp.sum(jnp.where(matches, slot_of[None, :], 0), axis=1)
    digits = jnp.stack([slot_ids // 64, slot_ids % 64]).astype(jnp.bfloat16)
    mine = lax.dynamic_slice_in_dim(embeddings, c * width, width, 1)
    packed = jnp.concatenate([mine, digits, jnp.zeros((14, width), jnp.bfloat16)], axis=0)
    others = [shifted(packed, "y", NY, d) for d in (2, 1, -1)]

    cent = copies(old_centroids.reshape(96, 128), NZ)
    cent = exchange(cent, ("zh", "zl"))

    widened = embeddings.astype(jnp.float32)
    root_mean = jnp.sqrt(jnp.mean(widened * widened, axis=1) + EPS)

    away = local_sums(y * 3 + (1 - zl) * (NY * 3), packed, others)
    arrived = shifted(away, "zl", ZL, 1)
    home = local_sums(y * 3 + zl * (NY * 3), packed, others)
    both = (home + arrived).reshape(ZH, NC * 3, width)
    summed = exchange(both, "zh")
    summed = summed.sum(axis=0)

    blocks = cent.reshape(NZ * 3, D)
    near = [shifted(blocks, "y", NY, d) for d in (1, -1)]
    far = shifted(blocks, "y", NY, 2)
    local = slot_ids - c * (NZ * NY * 3)
    owner = local // 3
    turn = (y - owner % NY) % NY
    place = jnp.where(turn == 0, 0, jnp.where(turn == 2, 1, jnp.where(turn == 1, 2, 3)))
    row_ids = place * (NZ * 3) + (owner // NY) * 3 + local % 3
    row_ids = jnp.where((local >= 0) & (local < NZ * NY * 3), row_ids, -1)
    partial = local_scores(row_ids[None, :], root_mean[None, :], [blocks, far, *near], embeddings)

    sends = jnp.concatenate(
        [summed.reshape(NC, 1, 3 * width), partial[:, None]], axis=2
    )
    got = exchange(sends, "c")[:, 0]
    distance = 1.0 - got[:, 3 * width :].sum(axis=0)
    own_sums = got[:, : 3 * width].reshape(NC, 3, width).swapaxes(0, 1).reshape(3, D)
    overall = own_sums + old_centroids.astype(jnp.float32)
    updated = overall * lax.rsqrt(jnp.mean(overall * overall, axis=1, keepdims=True) + EPS)
    return (updated, distance)


def solution(mesh):
    split = Mesh(mesh.devices.reshape(ZH, ZL, NY, NC), ("zh", "zl", "y", "c"))
    return jax.shard_map(
        steps,
        mesh=split,
        in_specs=(P(DP, None), P(DP), P(), P(CLUS_DP, None)),
        out_specs=(P(CLUS_DP, None), P(DP)),
        check_vma=False,
    )
```

```python
import jax
import jax.numpy as jnp
from jax import lax
from jax.experimental import pallas as pl
from jax.experimental.pallas import tpu as pltpu
from jax.sharding import Mesh
from jax.sharding import PartitionSpec as P


D = 4096
ZH, ZL, NY, NC = 8, 2, 4, 8
NZ = ZH * ZL
DP = ("zh", "zl", "y")
CLUS_DP = ("c", "zh", "zl", "y")
EPS = 1e-06


def shifted(x, axis, size, by):
    return lax.ppermute(x, axis, [(i, (i + by) % size) for i in range(size)])


def exchange(x, axis):
    return lax.all_to_all(x, axis, 0, 0, tiled=True)


def copies(x, count):
    return jnp.broadcast_to(x, (count, *x.shape))


def slot_column(rows, first):
    r = lax.broadcasted_iota(jnp.int32, (rows, 1), 0)
    per_z = NC * 3
    zh = r // per_z
    c = (r % per_z) // 3
    return c * (NZ * NY * 3) + zh * (ZL * NY * 3) + r % 3 + first


def id_row(ref, points):
    tail = ref[points : points + 16, :].astype(jnp.float32)
    return (tail[0:1, :] * 64.0 + tail[1:2, :]).astype(jnp.int32)


def sums_kernel(pos_ref, own_ref, a_ref, b_ref, c_ref, out_ref):
    points = own_ref.shape[0] - 16
    wanted = slot_column(out_ref.shape[0], pos_ref[0])
    total = None
    for ref in (own_ref, a_ref, b_ref, c_ref):
        hot = (wanted == id_row(ref, points)).astype(jnp.float32).astype(jnp.bfloat16)
        got = jnp.dot(hot, ref[0:points, :], preferred_element_type=jnp.float32)
        total = got if total is None else total + got
    out_ref[...] = total


def local_sums(first, own, others):
    rows = ZH * NC * 3
    width = own.shape[1]
    vmem = pl.BlockSpec(memory_space=pltpu.VMEM)
    return pl.pallas_call(
        sums_kernel,
        out_shape=jax.ShapeDtypeStruct((rows, width), jnp.float32),
        in_specs=[pl.BlockSpec(memory_space=pltpu.SMEM)] + [vmem] * 4,
        out_specs=vmem,
        name="local_sums",
    )(first.reshape(1), own, *others)


def score_kernel(pos_ref, own_ref, a_ref, b_ref, c_ref, here_ref, there_ref, keep_ref, give_ref):
    points = own_ref.shape[0] - 16
    parts = []
    for ref, first in ((here_ref, pos_ref[0]), (there_ref, pos_ref[1])):
        rows = ref[...]
        wide = rows.astype(jnp.float32)
        square = jnp.sum(wide * wide, axis=1, keepdims=True)
        parts.append((rows, square, slot_column(rows.shape[0], first)))
    for by, ref in enumerate((own_ref, a_ref, b_ref, c_ref)):
        ids = id_row(ref, points)
        score = size = None
        for rows, square, wanted in parts:
            raw = lax.dot_general(
                rows,
                ref[0:points, :],
                (((1,), (1,)), ((), ())),
                preferred_element_type=jnp.float32,
            )
            hit = wanted == ids
            got = jnp.sum(jnp.where(hit, raw, 0.0), axis=0, keepdims=True)
            more = jnp.sum(jnp.where(hit, square, 0.0), axis=0, keepdims=True)
            score = got if score is None else score + got
            size = more if size is None else size + more
        role = pos_ref[2 + by]
        for out_ref, wanted in ((keep_ref, role < 2), (give_ref, role >= 2)):

            @pl.when(wanted)
            def _(out_ref=out_ref, score=score, size=size, place=lax.rem(role, 2)):
                out_ref[place, 0:1, :] = score
                out_ref[place, 1:2, :] = size


def local_scores(firsts, own, others, here, there):
    points = own.shape[0] - 16
    vmem = pl.BlockSpec(memory_space=pltpu.VMEM)
    return pl.pallas_call(
        score_kernel,
        out_shape=(jax.ShapeDtypeStruct((2, 2, points), jnp.float32),) * 2,
        in_specs=[pl.BlockSpec(memory_space=pltpu.SMEM)] + [vmem] * 6,
        out_specs=(vmem, vmem),
        name="local_scores",
    )(firsts, own, *others, here, there)


def steps(embeddings, assignment, slot_of, old_centroids):
    points = embeddings.shape[0]
    clusters = slot_of.shape[0]
    width = D // NC
    c = lax.axis_index("c")
    y = lax.axis_index("y")
    zl = lax.axis_index("zl")

    matches = assignment[:, None] == jnp.arange(clusters, dtype=jnp.int32)[None, :]
    slot_ids = jnp.sum(jnp.where(matches, slot_of[None, :], 0), axis=1)
    digits = jnp.stack([slot_ids // 64, slot_ids % 64]).astype(jnp.bfloat16)
    mine = lax.dynamic_slice_in_dim(embeddings, c * width, width, 1)
    packed = jnp.concatenate([mine, digits, jnp.zeros((14, width), jnp.bfloat16)], axis=0)
    after, before = shifted(packed, "y", NY, -1), shifted(packed, "y", NY, 1)
    others = [after, shifted(packed, "y", NY, 2), before]
    cent = exchange(old_centroids.reshape(3, NC, width).swapaxes(0, 1), "c")

    here = exchange(copies(cent.reshape(NC * 3, width), ZH), "zh")
    here = here.reshape(ZH * NC * 3, width)

    widened = embeddings.astype(jnp.float32)
    root_mean = jnp.sqrt(jnp.mean(widened * widened, axis=1) + EPS)

    first_here = y * 3 + zl * (NY * 3)
    first_there = y * 3 + (1 - zl) * (NY * 3)
    away = local_sums(first_there, packed, others)
    arrived = shifted(away, "zl", ZL, 1)
    home = local_sums(first_here, packed, others)
    there = shifted(here, "zl", ZL, 1)
    both = (home + arrived).reshape(ZH, NC * 3, width)
    summed = exchange(both, "zh")
    summed = summed.sum(axis=0)

    sources = (y + jnp.arange(NY)) % NY
    roles = jnp.where(
        sources == y, 0, jnp.where(sources == 3 - y, 1, jnp.where(sources == (y ^ 1), 2, 3))
    )
    where = jnp.concatenate([jnp.stack([first_here, first_there]), roles]).astype(jnp.int32)
    keep, give = local_scores(where, packed, others, here, there)
    kept = keep + lax.ppermute(give, "y", [(0, 1), (1, 0), (2, 3), (3, 2)])
    scored = kept[0] + lax.ppermute(kept[1], "y", [(0, 3), (3, 0), (1, 2), (2, 1)])

    sends = jnp.concatenate(
        [
            summed.reshape(NC, 1, 3 * width),
            jnp.broadcast_to(scored.reshape(1, 1, 2 * points), (NC, 1, 2 * points)),
        ],
        axis=2,
    )
    got = exchange(sends, "c")[:, 0]
    both = got[:, 3 * width :].sum(axis=0)
    cent_rms = jnp.sqrt(both[points:] / jnp.float32(D) + EPS)
    distance = 1.0 - both[:points] / (jnp.float32(D) * root_mean * cent_rms)
    own_sums = got[:, : 3 * width].reshape(NC, 3, width).swapaxes(0, 1).reshape(3, D)
    overall = own_sums + old_centroids.astype(jnp.float32)
    updated = overall * lax.rsqrt(jnp.mean(overall * overall, axis=1, keepdims=True) + EPS)
    return (updated, distance)


def solution(mesh):
    split = Mesh(mesh.devices.reshape(ZH, ZL, NY, NC), ("zh", "zl", "y", "c"))
    return jax.shard_map(
        steps,
        mesh=split,
        in_specs=(P(DP, None), P(DP), P(), P(CLUS_DP, None)),
        out_specs=(P(CLUS_DP, None), P(DP)),
        check_vma=False,
    )
```

```python
import functools

import jax
import jax.numpy as jnp
from jax import lax
from jax.experimental import pallas as pl
from jax.experimental.pallas import tpu as pltpu
from jax.sharding import Mesh
from jax.sharding import PartitionSpec as P


D = 4096
ZH, ZL, NY, NC = 8, 2, 4, 8
NZ = ZH * ZL
DP = ("zh", "zl", "y")
CLUS_DP = ("c", "zh", "zl", "y")
EPS = 1e-06


def shifted(x, axis, size, by):
    return lax.ppermute(x, axis, [(i, (i + by) % size) for i in range(size)])


def exchange(x, axis):
    return lax.all_to_all(x, axis, 0, 0, tiled=True)


def copies(x, count):
    return jnp.broadcast_to(x, (count, *x.shape))


LIMIT = pltpu.CompilerParams(vmem_limit_bytes=12 * 1024 * 1024)


def near(x):
    return pltpu.with_memory_space_constraint(x, pltpu.VMEM)


def far(x):
    return pltpu.with_memory_space_constraint(x, pltpu.HBM)


def pack_kernel(pos_ref, ids_ref, table_ref, emb_ref, out_ref, rows_ref, in_ref, list_ref, sems):
    points, width = emb_ref.shape[0], out_ref.shape[1]
    start = pl.multiple_of(pos_ref[2] * width, width)
    copy = pltpu.make_async_copy(
        emb_ref.at[:, pl.ds(start, width)], out_ref.at[pl.ds(0, points), :], sems.at[0]
    )
    copy.start()
    small = [
        pltpu.make_async_copy(ids_ref, in_ref, sems.at[1]),
        pltpu.make_async_copy(table_ref, list_ref, sems.at[2]),
    ]
    for each in small:
        each.start()
    for each in small:
        each.wait()
    groups = table_ref.shape[0] // 128
    rows_ref[...] = jnp.zeros(rows_ref.shape, jnp.float32)
    for g in range(groups):
        slots = list_ref[g * 128 : (g + 1) * 128].reshape(1, 128)
        rows_ref[g : g + 1, :] = lax.shift_right_logical(slots, 6).astype(jnp.float32)
        rows_ref[16 + g : 17 + g, :] = (slots & 63).astype(jnp.float32)
    ids = in_ref[...]
    low = lax.broadcasted_iota(jnp.int32, (128, points), 0) == (ids & 127)
    got = jnp.dot(
        rows_ref[...].astype(jnp.bfloat16),
        low.astype(jnp.float32).astype(jnp.bfloat16),
        preferred_element_type=jnp.float32,
    )
    high = lax.broadcasted_iota(jnp.int32, (16, points), 0)
    chosen = high == lax.shift_right_logical(ids, 7)
    coarse = jnp.sum(jnp.where(chosen, got[:16], 0.0), axis=0, keepdims=True)
    fine = jnp.sum(jnp.where(chosen, got[16:], 0.0), axis=0, keepdims=True)
    tail = jnp.where(high == 0, coarse, jnp.where(high == 1, fine, 0.0))
    out_ref[points : points + 16, :] = tail.astype(jnp.bfloat16)
    copy.wait()


def pack(pos, assignment, slot_of, embeddings):
    points, width = embeddings.shape[0], D // NC
    vmem = pl.BlockSpec(memory_space=pltpu.VMEM)
    return pl.pallas_call(
        pack_kernel,
        out_shape=jax.ShapeDtypeStruct((points + 16, width), jnp.bfloat16),
        in_specs=[pl.BlockSpec(memory_space=pltpu.SMEM)]
        + [pl.BlockSpec(memory_space=pltpu.HBM)] * 3,
        out_specs=vmem,
        scratch_shapes=[
            pltpu.VMEM((32, 128), jnp.float32),
            pltpu.VMEM((1, points), jnp.int32),
            pltpu.VMEM(slot_of.shape, jnp.int32),
            pltpu.SemaphoreType.DMA((3,)),
        ],
        compiler_params=LIMIT,
        name="pack",
    )(pos, *map(far, (assignment[None, :], slot_of, embeddings)))


def ending_kernel(got_ref, old_ref, new_ref, dist_ref):
    width = D // NC
    points = dist_ref.shape[1]
    old = old_ref[...].astype(jnp.float32)
    for c in range(NC):
        for k in range(3):
            new_ref[k : k + 1, c * width : (c + 1) * width] = got_ref[
                c : c + 1, k * width : (k + 1) * width
            ]
    overall = new_ref[...] + old
    size = jnp.mean(overall * overall, axis=1, keepdims=True)
    new_ref[...] = overall * lax.rsqrt(size + EPS)
    scores = jnp.sum(got_ref[:, 3 * width :], axis=0, keepdims=True)
    cent_rms = jnp.sqrt(scores[:, points : 2 * points] / jnp.float32(D) + EPS)
    root_mean = jnp.sqrt(scores[:, 2 * points :] / jnp.float32(D) + EPS)
    dist_ref[...] = 1.0 - scores[:, :points] / (jnp.float32(D) * root_mean * cent_rms)


def ending(got, old, points):
    vmem = pl.BlockSpec(memory_space=pltpu.VMEM)
    return pl.pallas_call(
        ending_kernel,
        out_shape=(
            jax.ShapeDtypeStruct(old.shape, jnp.float32),
            jax.ShapeDtypeStruct((1, points), jnp.float32),
        ),
        in_specs=[vmem, vmem],
        out_specs=(vmem, vmem),
        compiler_params=LIMIT,
        name="ending",
    )(near(got), near(old))


def slot_column(rows, pos_ref, partner):
    r = lax.broadcasted_iota(jnp.int32, (rows, 1), 0)
    per_z = NC * 3
    zh = r // per_z
    c = (r % per_z) // 3
    half = 1 - pos_ref[1] if partner else pos_ref[1]
    first = (half * NY + pos_ref[0]) * 3
    return c * (NZ * NY * 3) + zh * (ZL * NY * 3) + r % 3 + first


def id_row(ref, points):
    tail = ref[points : points + 16, :].astype(jnp.float32)
    return (tail[0:1, :] * 64.0 + tail[1:2, :]).astype(jnp.int32)


def sums_kernel(partner, pos_ref, own_ref, a_ref, b_ref, c_ref, *out_refs):
    points = own_ref.shape[0] - 16
    wanted = slot_column(out_refs[0].shape[0], pos_ref, partner)
    total = None
    for ref in (own_ref, a_ref, b_ref, c_ref):
        hot = (wanted == id_row(ref, points)).astype(jnp.float32).astype(jnp.bfloat16)
        got = jnp.dot(hot, ref[0:points, :], preferred_element_type=jnp.float32)
        total = got if total is None else total + got
    width = out_refs[0].shape[1]
    for i, out_ref in enumerate(out_refs):
        out_ref[...] = total[:, i * width : (i + 1) * width]


def local_sums(pos, own, others, cuts, partner):
    rows = ZH * NC * 3
    width = own.shape[1] // cuts
    vmem = pl.BlockSpec(memory_space=pltpu.VMEM)
    return pl.pallas_call(
        functools.partial(sums_kernel, partner),
        out_shape=(jax.ShapeDtypeStruct((rows, width), jnp.float32),) * cuts,
        in_specs=[pl.BlockSpec(memory_space=pltpu.SMEM)] + [vmem] * 4,
        out_specs=(vmem,) * cuts,
        compiler_params=LIMIT,
        name="local_sums",
    )(pos, *map(near, (own, *others)))


def merge_kernel(home_ref, a_ref, b_ref, out_ref):
    width = a_ref.shape[1]
    out_ref[:, :width] = home_ref[:, :width] + a_ref[...]
    out_ref[:, width:] = home_ref[:, width:] + b_ref[...]


def merged(home, a, b):
    vmem = pl.BlockSpec(memory_space=pltpu.VMEM)
    return pl.pallas_call(
        merge_kernel,
        out_shape=jax.ShapeDtypeStruct(home.shape, jnp.float32),
        in_specs=[vmem] * 3,
        out_specs=vmem,
        compiler_params=LIMIT,
        name="merged",
    )(*map(near, (home, a, b)))


def score_kernel(pos_ref, own_ref, a_ref, b_ref, c_ref, here_ref, there_ref, keep_ref, give_ref, size_ref):
    points = own_ref.shape[0] - 16
    wide = own_ref[0:points, :].astype(jnp.float32)
    wide = wide * wide
    high = wide.astype(jnp.bfloat16)
    low = (wide - high.astype(jnp.float32)).astype(jnp.bfloat16)
    ones = jnp.ones((16, wide.shape[1]), jnp.bfloat16)
    across = (((1,), (1,)), ((), ()))
    sizes = [
        lax.dot_general(ones, part, across, preferred_element_type=jnp.float32)
        for part in (high, low)
    ]
    size_ref[...] = (sizes[0] + sizes[1])[0:1, :]
    parts = []
    for partner, ref in enumerate((here_ref, there_ref)):
        rows = ref[...]
        wide = rows.astype(jnp.float32)
        square = jnp.sum(wide * wide, axis=1, keepdims=True)
        parts.append((rows, square, slot_column(rows.shape[0], pos_ref, partner)))
    for by, ref in enumerate((own_ref, a_ref, b_ref, c_ref)):
        ids = id_row(ref, points)
        score = size = None
        for rows, square, wanted in parts:
            raw = lax.dot_general(
                rows,
                ref[0:points, :],
                (((1,), (1,)), ((), ())),
                preferred_element_type=jnp.float32,
            )
            hit = wanted == ids
            got = jnp.sum(jnp.where(hit, raw, 0.0), axis=0, keepdims=True)
            more = jnp.sum(jnp.where(hit, square, 0.0), axis=0, keepdims=True)
            score = got if score is None else score + got
            size = more if size is None else size + more
        y = pos_ref[0]
        source = lax.rem(y + by, NY)
        beside = y + 1 - 2 * lax.rem(y, 2)
        role = jnp.where(
            source == y, 0, jnp.where(source == 3 - y, 1, jnp.where(source == beside, 2, 3))
        )
        for out_ref, wanted in ((keep_ref, role < 2), (give_ref, role >= 2)):

            @pl.when(wanted)
            def _(out_ref=out_ref, score=score, size=size, place=lax.rem(role, 2)):
                out_ref[place, 0:1, :] = score
                out_ref[place, 1:2, :] = size


def local_scores(pos, own, others, here, there):
    points = own.shape[0] - 16
    vmem = pl.BlockSpec(memory_space=pltpu.VMEM)
    return pl.pallas_call(
        score_kernel,
        out_shape=(jax.ShapeDtypeStruct((2, 2, points), jnp.float32),) * 2
        + (jax.ShapeDtypeStruct((1, points), jnp.float32),),
        in_specs=[pl.BlockSpec(memory_space=pltpu.SMEM)] + [vmem] * 6,
        out_specs=(vmem,) * 3,
        compiler_params=LIMIT,
        name="local_scores",
    )(pos, *map(near, (own, *others, here, there)))


def steps(embeddings, assignment, slot_of, old_centroids):
    points = embeddings.shape[0]
    width = D // NC
    c = lax.axis_index("c")
    y = lax.axis_index("y")
    zl = lax.axis_index("zl")

    pos = jnp.stack([y, zl, c]).astype(jnp.int32)
    packed = pack(pos, assignment, slot_of, embeddings)
    far = shifted(packed, "y", NY, 2)
    after = shifted(packed, "y", NY, -1)
    before = shifted(packed, "y", NY, 1)
    others = [after, far, before]
    cent = exchange(old_centroids.reshape(3, NC, width).swapaxes(0, 1), "c")

    here = exchange(copies(cent.reshape(NC * 3, width), ZH), "zh")
    here = here.reshape(ZH * NC * 3, width)

    away = local_sums(pos, packed, others, 2, True)
    beside = [(z, (z - 1 if z % ZL == 0 else z + 1) % NZ) for z in range(NZ)]
    arrived = shifted(away[0], "zl", ZL, 1), lax.ppermute(away[1], ("zh", "zl"), beside)
    (home,) = local_sums(pos, packed, others, 1, False)
    there = lax.ppermute(here, ("zh", "zl"), beside)
    both = merged(home, *arrived).reshape(ZH, NC * 3, width)
    summed = exchange(both, "zh")
    summed = summed.sum(axis=0)

    keep, give, size = local_scores(pos, packed, others, here, there)
    kept = keep + lax.ppermute(give, "y", [(0, 1), (1, 0), (2, 3), (3, 2)])
    scored = kept[0] + lax.ppermute(kept[1], "y", [(0, 3), (3, 0), (1, 2), (2, 1)])

    sends = jnp.concatenate(
        [
            summed.reshape(NC, 1, 3 * width),
            jnp.broadcast_to(scored.reshape(1, 1, 2 * points), (NC, 1, 2 * points)),
            jnp.broadcast_to(size[None], (NC, 1, points)),
        ],
        axis=2,
    )
    got = exchange(sends, "c")[:, 0]
    updated, distance = ending(got, old_centroids, points)
    return (updated, distance[0])


def solution(mesh):
    split = Mesh(mesh.devices.reshape(ZH, ZL, NY, NC), ("zh", "zl", "y", "c"))
    return jax.shard_map(
        steps,
        mesh=split,
        in_specs=(P(DP, None), P(DP), P(), P(CLUS_DP, None)),
        out_specs=(P(CLUS_DP, None), P(DP)),
        check_vma=False,
    )
```

```python
import functools

import jax
import jax.numpy as jnp
from jax import lax
from jax.experimental import pallas as pl
from jax.experimental.pallas import tpu as pltpu
from jax.sharding import Mesh
from jax.sharding import PartitionSpec as P


D = 4096
ZH, ZL, NY, NC = 8, 2, 4, 8
NZ = ZH * ZL
DP = ("zh", "zl", "y")
CLUS_DP = ("c", "zh", "zl", "y")
EPS = 1e-06


def shifted(x, axis, size, by):
    return lax.ppermute(x, axis, [(i, (i + by) % size) for i in range(size)])


def exchange(x, axis, order=None):
    groups = None if order is None else [list(order)]
    return lax.all_to_all(x, axis, 0, 0, tiled=True, axis_index_groups=groups)


def copies(x, count):
    return jnp.broadcast_to(x, (count, *x.shape))


ROW_TURN = 4
SUM_TURN = 4


def turned(by):
    return [(i + by) % ZH for i in range(ZH)]


LIMIT = pltpu.CompilerParams(vmem_limit_bytes=12 * 1024 * 1024)


def near(x):
    return pltpu.with_memory_space_constraint(x, pltpu.VMEM)


def far(x):
    return pltpu.with_memory_space_constraint(x, pltpu.HBM)


def pack_kernel(pos_ref, ids_ref, table_ref, emb_ref, out_ref, rows_ref, in_ref, list_ref, sems):
    points, width = emb_ref.shape[0], out_ref.shape[1]
    start = pl.multiple_of(pos_ref[2] * width, width)
    copy = pltpu.make_async_copy(
        emb_ref.at[:, pl.ds(start, width)], out_ref.at[pl.ds(0, points), :], sems.at[0]
    )
    copy.start()
    small = [
        pltpu.make_async_copy(ids_ref, in_ref, sems.at[1]),
        pltpu.make_async_copy(table_ref, list_ref, sems.at[2]),
    ]
    for each in small:
        each.start()
    for each in small:
        each.wait()
    groups = table_ref.shape[0] // 128
    rows_ref[...] = jnp.zeros(rows_ref.shape, jnp.float32)
    for g in range(groups):
        slots = list_ref[g * 128 : (g + 1) * 128].reshape(1, 128)
        rows_ref[g : g + 1, :] = lax.shift_right_logical(slots, 6).astype(jnp.float32)
        rows_ref[16 + g : 17 + g, :] = (slots & 63).astype(jnp.float32)
    ids = in_ref[...]
    low = lax.broadcasted_iota(jnp.int32, (128, points), 0) == (ids & 127)
    got = jnp.dot(
        rows_ref[...].astype(jnp.bfloat16),
        low.astype(jnp.float32).astype(jnp.bfloat16),
        preferred_element_type=jnp.float32,
    )
    high = lax.broadcasted_iota(jnp.int32, (16, points), 0)
    chosen = high == lax.shift_right_logical(ids, 7)
    coarse = jnp.sum(jnp.where(chosen, got[:16], 0.0), axis=0, keepdims=True)
    fine = jnp.sum(jnp.where(chosen, got[16:], 0.0), axis=0, keepdims=True)
    tail = jnp.where(high == 0, coarse, jnp.where(high == 1, fine, 0.0))
    out_ref[points : points + 16, :] = tail.astype(jnp.bfloat16)
    copy.wait()


def pack(pos, assignment, slot_of, embeddings):
    points, width = embeddings.shape[0], D // NC
    vmem = pl.BlockSpec(memory_space=pltpu.VMEM)
    return pl.pallas_call(
        pack_kernel,
        out_shape=jax.ShapeDtypeStruct((points + 16, width), jnp.bfloat16),
        in_specs=[pl.BlockSpec(memory_space=pltpu.SMEM)]
        + [pl.BlockSpec(memory_space=pltpu.HBM)] * 3,
        out_specs=vmem,
        scratch_shapes=[
            pltpu.VMEM((32, 128), jnp.float32),
            pltpu.VMEM((1, points), jnp.int32),
            pltpu.VMEM(slot_of.shape, jnp.int32),
            pltpu.SemaphoreType.DMA((3,)),
        ],
        compiler_params=LIMIT,
        name="pack",
    )(pos, *map(far, (assignment[None, :], slot_of, embeddings)))


def ending_kernel(got_ref, old_ref, new_ref, dist_ref):
    width = D // NC
    points = dist_ref.shape[1]
    old = old_ref[...].astype(jnp.float32)
    for c in range(NC):
        for k in range(3):
            new_ref[k : k + 1, c * width : (c + 1) * width] = got_ref[
                c : c + 1, k * width : (k + 1) * width
            ]
    overall = new_ref[...] + old
    size = jnp.mean(overall * overall, axis=1, keepdims=True)
    new_ref[...] = overall * lax.rsqrt(size + EPS)
    scores = jnp.sum(got_ref[:, 3 * width :], axis=0, keepdims=True)
    cent_rms = jnp.sqrt(scores[:, points : 2 * points] / jnp.float32(D) + EPS)
    root_mean = jnp.sqrt(scores[:, 2 * points :] / jnp.float32(D) + EPS)
    dist_ref[...] = 1.0 - scores[:, :points] / (jnp.float32(D) * root_mean * cent_rms)


def ending(got, old, points):
    vmem = pl.BlockSpec(memory_space=pltpu.VMEM)
    return pl.pallas_call(
        ending_kernel,
        out_shape=(
            jax.ShapeDtypeStruct(old.shape, jnp.float32),
            jax.ShapeDtypeStruct((1, points), jnp.float32),
        ),
        in_specs=[vmem, vmem],
        out_specs=(vmem, vmem),
        compiler_params=LIMIT,
        name="ending",
    )(near(got), near(old))


def slot_column(rows, pos_ref, partner, turn):
    r = lax.broadcasted_iota(jnp.int32, (rows, 1), 0)
    per_z = NC * 3
    zh = (r // per_z + turn) % ZH
    c = (r % per_z) // 3
    half = 1 - pos_ref[1] if partner else pos_ref[1]
    first = (half * NY + pos_ref[0]) * 3
    return c * (NZ * NY * 3) + zh * (ZL * NY * 3) + r % 3 + first


def id_row(ref, points):
    tail = ref[points : points + 16, :].astype(jnp.float32)
    return (tail[0:1, :] * 64.0 + tail[1:2, :]).astype(jnp.int32)


def sums_kernel(partner, pos_ref, own_ref, a_ref, b_ref, c_ref, *out_refs):
    points = own_ref.shape[0] - 16
    wanted = slot_column(out_refs[0].shape[0], pos_ref, partner, SUM_TURN)
    total = None
    for ref in (own_ref, a_ref, b_ref, c_ref):
        hot = (wanted == id_row(ref, points)).astype(jnp.float32).astype(jnp.bfloat16)
        got = jnp.dot(hot, ref[0:points, :], preferred_element_type=jnp.float32)
        total = got if total is None else total + got
    width = out_refs[0].shape[1]
    for i, out_ref in enumerate(out_refs):
        out_ref[...] = total[:, i * width : (i + 1) * width]


def local_sums(pos, own, others, cuts, partner):
    rows = ZH * NC * 3
    width = own.shape[1] // cuts
    vmem = pl.BlockSpec(memory_space=pltpu.VMEM)
    return pl.pallas_call(
        functools.partial(sums_kernel, partner),
        out_shape=(jax.ShapeDtypeStruct((rows, width), jnp.float32),) * cuts,
        in_specs=[pl.BlockSpec(memory_space=pltpu.SMEM)] + [vmem] * 4,
        out_specs=(vmem,) * cuts,
        compiler_params=LIMIT,
        name="local_sums",
    )(pos, *map(near, (own, *others)))


def merge_kernel(home_ref, a_ref, b_ref, out_ref):
    width = a_ref.shape[1]
    out_ref[:, :width] = home_ref[:, :width] + a_ref[...]
    out_ref[:, width:] = home_ref[:, width:] + b_ref[...]


def merged(home, a, b):
    vmem = pl.BlockSpec(memory_space=pltpu.VMEM)
    return pl.pallas_call(
        merge_kernel,
        out_shape=jax.ShapeDtypeStruct(home.shape, jnp.float32),
        in_specs=[vmem] * 3,
        out_specs=vmem,
        compiler_params=LIMIT,
        name="merged",
    )(*map(near, (home, a, b)))


def score_kernel(pos_ref, own_ref, a_ref, b_ref, c_ref, here_ref, there_ref, keep_ref, give_ref, size_ref):
    points = own_ref.shape[0] - 16
    wide = own_ref[0:points, :].astype(jnp.float32)
    wide = wide * wide
    high = wide.astype(jnp.bfloat16)
    low = (wide - high.astype(jnp.float32)).astype(jnp.bfloat16)
    ones = jnp.ones((16, wide.shape[1]), jnp.bfloat16)
    across = (((1,), (1,)), ((), ()))
    sizes = [
        lax.dot_general(ones, part, across, preferred_element_type=jnp.float32)
        for part in (high, low)
    ]
    size_ref[...] = (sizes[0] + sizes[1])[0:1, :]
    parts = []
    for partner, ref in enumerate((here_ref, there_ref)):
        rows = ref[...]
        wide = rows.astype(jnp.float32)
        square = jnp.sum(wide * wide, axis=1, keepdims=True)
        parts.append((rows, square, slot_column(rows.shape[0], pos_ref, partner, ROW_TURN)))
    for by, ref in enumerate((own_ref, a_ref, b_ref, c_ref)):
        ids = id_row(ref, points)
        score = size = None
        for rows, square, wanted in parts:
            raw = lax.dot_general(
                rows,
                ref[0:points, :],
                (((1,), (1,)), ((), ())),
                preferred_element_type=jnp.float32,
            )
            hit = wanted == ids
            got = jnp.sum(jnp.where(hit, raw, 0.0), axis=0, keepdims=True)
            more = jnp.sum(jnp.where(hit, square, 0.0), axis=0, keepdims=True)
            score = got if score is None else score + got
            size = more if size is None else size + more
        y = pos_ref[0]
        source = lax.rem(y + by, NY)
        beside = y + 1 - 2 * lax.rem(y, 2)
        role = jnp.where(
            source == y, 0, jnp.where(source == 3 - y, 1, jnp.where(source == beside, 2, 3))
        )
        for out_ref, wanted in ((keep_ref, role < 2), (give_ref, role >= 2)):

            @pl.when(wanted)
            def _(out_ref=out_ref, score=score, size=size, place=lax.rem(role, 2)):
                out_ref[place, 0:1, :] = score
                out_ref[place, 1:2, :] = size


def local_scores(pos, own, others, here, there):
    points = own.shape[0] - 16
    vmem = pl.BlockSpec(memory_space=pltpu.VMEM)
    return pl.pallas_call(
        score_kernel,
        out_shape=(jax.ShapeDtypeStruct((2, 2, points), jnp.float32),) * 2
        + (jax.ShapeDtypeStruct((1, points), jnp.float32),),
        in_specs=[pl.BlockSpec(memory_space=pltpu.SMEM)] + [vmem] * 6,
        out_specs=(vmem,) * 3,
        compiler_params=LIMIT,
        name="local_scores",
    )(pos, *map(near, (own, *others, here, there)))


def steps(embeddings, assignment, slot_of, old_centroids):
    points = embeddings.shape[0]
    width = D // NC
    c = lax.axis_index("c")
    y = lax.axis_index("y")
    zl = lax.axis_index("zl")

    pos = jnp.stack([y, zl, c]).astype(jnp.int32)
    packed = pack(pos, assignment, slot_of, embeddings)
    far = shifted(packed, "y", NY, 2)
    after = shifted(packed, "y", NY, -1)
    before = shifted(packed, "y", NY, 1)
    others = [after, far, before]
    cent = exchange(old_centroids.reshape(3, NC, width).swapaxes(0, 1), "c")

    here = exchange(copies(cent.reshape(NC * 3, width), ZH), "zh", turned(ROW_TURN))
    here = here.reshape(ZH * NC * 3, width)

    away = local_sums(pos, packed, others, 2, True)
    beside = [(z, (z - 1 if z % ZL == 0 else z + 1) % NZ) for z in range(NZ)]
    arrived = shifted(away[0], "zl", ZL, 1), lax.ppermute(away[1], ("zh", "zl"), beside)
    (home,) = local_sums(pos, packed, others, 1, False)
    there = lax.ppermute(here, ("zh", "zl"), beside)
    both = merged(home, *arrived).reshape(ZH, NC * 3, width)
    summed = exchange(both, "zh", turned(SUM_TURN))
    summed = summed.sum(axis=0)

    keep, give, size = local_scores(pos, packed, others, here, there)
    kept = keep + lax.ppermute(give, "y", [(0, 1), (1, 0), (2, 3), (3, 2)])
    scored = kept[0] + lax.ppermute(kept[1], "y", [(0, 3), (3, 0), (1, 2), (2, 1)])

    sends = jnp.concatenate(
        [
            summed.reshape(NC, 1, 3 * width),
            jnp.broadcast_to(scored.reshape(1, 1, 2 * points), (NC, 1, 2 * points)),
            jnp.broadcast_to(size[None], (NC, 1, points)),
        ],
        axis=2,
    )
    got = exchange(sends, "c")[:, 0]
    updated, distance = ending(got, old_centroids, points)
    return (updated, distance[0])


def solution(mesh):
    split = Mesh(mesh.devices.reshape(ZH, ZL, NY, NC), ("zh", "zl", "y", "c"))
    return jax.shard_map(
        steps,
        mesh=split,
        in_specs=(P(DP, None), P(DP), P(), P(CLUS_DP, None)),
        out_specs=(P(CLUS_DP, None), P(DP)),
        check_vma=False,
    )
```

```python
import functools

import jax
import jax.numpy as jnp
from jax import lax
from jax.experimental import pallas as pl
from jax.experimental.pallas import tpu as pltpu
from jax.sharding import Mesh
from jax.sharding import PartitionSpec as P


D = 4096
ZH, ZL, NY, NC = 8, 2, 4, 8
NZ = ZH * ZL
DP = ("zh", "zl", "y")
CLUS_DP = ("c", "zh", "zl", "y")
EPS = 1e-06


def shifted(x, axis, size, by):
    return lax.ppermute(x, axis, [(i, (i + by) % size) for i in range(size)])


def exchange(x, axis, order=None):
    groups = None if order is None else [list(order)]
    return lax.all_to_all(x, axis, 0, 0, tiled=True, axis_index_groups=groups)


def copies(x, count):
    return jnp.broadcast_to(x, (count, *x.shape))


ROW_TURN = 4
SUM_TURN = 4
WHOLE_TURN = 4


def turned(by):
    return [(i + by) % 8 for i in range(8)]


LIMIT = pltpu.CompilerParams(vmem_limit_bytes=12 * 1024 * 1024)


def near(x):
    return pltpu.with_memory_space_constraint(x, pltpu.VMEM)


def far(x):
    return pltpu.with_memory_space_constraint(x, pltpu.HBM)


def pack_kernel(pos_ref, ids_ref, table_ref, emb_ref, out_ref, rows_ref, in_ref, list_ref, sems):
    points, width = emb_ref.shape[0], out_ref.shape[1]
    start = pl.multiple_of(pos_ref[2] * width, width)
    copy = pltpu.make_async_copy(
        emb_ref.at[:, pl.ds(start, width)], out_ref.at[pl.ds(0, points), :], sems.at[0]
    )
    copy.start()
    small = [
        pltpu.make_async_copy(ids_ref, in_ref, sems.at[1]),
        pltpu.make_async_copy(table_ref, list_ref, sems.at[2]),
    ]
    for each in small:
        each.start()
    for each in small:
        each.wait()
    groups = table_ref.shape[0] // 128
    rows_ref[...] = jnp.zeros(rows_ref.shape, jnp.float32)
    for g in range(groups):
        slots = list_ref[g * 128 : (g + 1) * 128].reshape(1, 128)
        rows_ref[g : g + 1, :] = lax.shift_right_logical(slots, 6).astype(jnp.float32)
        rows_ref[16 + g : 17 + g, :] = (slots & 63).astype(jnp.float32)
    ids = in_ref[...]
    low = lax.broadcasted_iota(jnp.int32, (128, points), 0) == (ids & 127)
    got = jnp.dot(
        rows_ref[...].astype(jnp.bfloat16),
        low.astype(jnp.float32).astype(jnp.bfloat16),
        preferred_element_type=jnp.float32,
    )
    high = lax.broadcasted_iota(jnp.int32, (16, points), 0)
    chosen = high == lax.shift_right_logical(ids, 7)
    coarse = jnp.sum(jnp.where(chosen, got[:16], 0.0), axis=0, keepdims=True)
    fine = jnp.sum(jnp.where(chosen, got[16:], 0.0), axis=0, keepdims=True)
    tail = jnp.where(high == 0, coarse, jnp.where(high == 1, fine, 0.0))
    out_ref[points : points + 16, :] = tail.astype(jnp.bfloat16)
    copy.wait()


def pack(pos, assignment, slot_of, embeddings):
    points, width = embeddings.shape[0], D // NC
    vmem = pl.BlockSpec(memory_space=pltpu.VMEM)
    return pl.pallas_call(
        pack_kernel,
        out_shape=jax.ShapeDtypeStruct((points + 16, width), jnp.bfloat16),
        in_specs=[pl.BlockSpec(memory_space=pltpu.SMEM)]
        + [pl.BlockSpec(memory_space=pltpu.HBM)] * 3,
        out_specs=vmem,
        scratch_shapes=[
            pltpu.VMEM((32, 128), jnp.float32),
            pltpu.VMEM((1, points), jnp.int32),
            pltpu.VMEM(slot_of.shape, jnp.int32),
            pltpu.SemaphoreType.DMA((3,)),
        ],
        compiler_params=LIMIT,
        name="pack",
    )(pos, *map(far, (assignment[None, :], slot_of, embeddings)))


def ending_kernel(got_ref, old_ref, new_ref, dist_ref):
    width = D // NC
    points = dist_ref.shape[1]
    old = old_ref[...].astype(jnp.float32)
    for i in range(NC):
        c = (i + WHOLE_TURN) % NC
        for k in range(3):
            new_ref[k : k + 1, c * width : (c + 1) * width] = got_ref[
                i : i + 1, k * width : (k + 1) * width
            ]
    overall = new_ref[...] + old
    size = jnp.mean(overall * overall, axis=1, keepdims=True)
    new_ref[...] = overall * lax.rsqrt(size + EPS)
    scores = jnp.sum(got_ref[:, 3 * width :], axis=0, keepdims=True)
    cent_rms = jnp.sqrt(scores[:, points : 2 * points] / jnp.float32(D) + EPS)
    root_mean = jnp.sqrt(scores[:, 2 * points :] / jnp.float32(D) + EPS)
    dist_ref[...] = 1.0 - scores[:, :points] / (jnp.float32(D) * root_mean * cent_rms)


def ending(got, old, points):
    vmem = pl.BlockSpec(memory_space=pltpu.VMEM)
    return pl.pallas_call(
        ending_kernel,
        out_shape=(
            jax.ShapeDtypeStruct(old.shape, jnp.float32),
            jax.ShapeDtypeStruct((1, points), jnp.float32),
        ),
        in_specs=[vmem, vmem],
        out_specs=(vmem, vmem),
        compiler_params=LIMIT,
        name="ending",
    )(near(got), near(old))


def slot_column(rows, pos_ref, partner, turn, c_turn):
    r = lax.broadcasted_iota(jnp.int32, (rows, 1), 0)
    per_z = NC * 3
    zh = (r // per_z + turn) % ZH
    c = ((r % per_z) // 3 + c_turn) % NC
    half = 1 - pos_ref[1] if partner else pos_ref[1]
    first = (half * NY + pos_ref[0]) * 3
    return c * (NZ * NY * 3) + zh * (ZL * NY * 3) + r % 3 + first


def id_row(ref, points):
    tail = ref[points : points + 16, :].astype(jnp.float32)
    return (tail[0:1, :] * 64.0 + tail[1:2, :]).astype(jnp.int32)


def sums_kernel(partner, pos_ref, own_ref, a_ref, b_ref, c_ref, *out_refs):
    points = own_ref.shape[0] - 16
    wanted = slot_column(out_refs[0].shape[0], pos_ref, partner, SUM_TURN, WHOLE_TURN)
    total = None
    for ref in (own_ref, a_ref, b_ref, c_ref):
        hot = (wanted == id_row(ref, points)).astype(jnp.float32).astype(jnp.bfloat16)
        got = jnp.dot(hot, ref[0:points, :], preferred_element_type=jnp.float32)
        total = got if total is None else total + got
    width = out_refs[0].shape[1]
    for i, out_ref in enumerate(out_refs):
        out_ref[...] = total[:, i * width : (i + 1) * width]


def local_sums(pos, own, others, cuts, partner):
    rows = ZH * NC * 3
    width = own.shape[1] // cuts
    vmem = pl.BlockSpec(memory_space=pltpu.VMEM)
    return pl.pallas_call(
        functools.partial(sums_kernel, partner),
        out_shape=(jax.ShapeDtypeStruct((rows, width), jnp.float32),) * cuts,
        in_specs=[pl.BlockSpec(memory_space=pltpu.SMEM)] + [vmem] * 4,
        out_specs=(vmem,) * cuts,
        compiler_params=LIMIT,
        name="local_sums",
    )(pos, *map(near, (own, *others)))


def merge_kernel(home_ref, a_ref, b_ref, out_ref):
    width = a_ref.shape[1]
    out_ref[:, :width] = home_ref[:, :width] + a_ref[...]
    out_ref[:, width:] = home_ref[:, width:] + b_ref[...]


def merged(home, a, b):
    vmem = pl.BlockSpec(memory_space=pltpu.VMEM)
    return pl.pallas_call(
        merge_kernel,
        out_shape=jax.ShapeDtypeStruct(home.shape, jnp.float32),
        in_specs=[vmem] * 3,
        out_specs=vmem,
        compiler_params=LIMIT,
        name="merged",
    )(*map(near, (home, a, b)))


def score_kernel(pos_ref, own_ref, a_ref, b_ref, c_ref, here_ref, there_ref, keep_ref, give_ref, size_ref):
    points = own_ref.shape[0] - 16
    wide = own_ref[0:points, :].astype(jnp.float32)
    wide = wide * wide
    high = wide.astype(jnp.bfloat16)
    low = (wide - high.astype(jnp.float32)).astype(jnp.bfloat16)
    ones = jnp.ones((16, wide.shape[1]), jnp.bfloat16)
    across = (((1,), (1,)), ((), ()))
    sizes = [
        lax.dot_general(ones, part, across, preferred_element_type=jnp.float32)
        for part in (high, low)
    ]
    size_ref[...] = (sizes[0] + sizes[1])[0:1, :]
    parts = []
    for partner, ref in enumerate((here_ref, there_ref)):
        rows = ref[...]
        wide = rows.astype(jnp.float32)
        square = jnp.sum(wide * wide, axis=1, keepdims=True)
        parts.append((rows, square, slot_column(rows.shape[0], pos_ref, partner, ROW_TURN, 0)))
    for by, ref in enumerate((own_ref, a_ref, b_ref, c_ref)):
        ids = id_row(ref, points)
        score = size = None
        for rows, square, wanted in parts:
            raw = lax.dot_general(
                rows,
                ref[0:points, :],
                (((1,), (1,)), ((), ())),
                preferred_element_type=jnp.float32,
            )
            hit = wanted == ids
            got = jnp.sum(jnp.where(hit, raw, 0.0), axis=0, keepdims=True)
            more = jnp.sum(jnp.where(hit, square, 0.0), axis=0, keepdims=True)
            score = got if score is None else score + got
            size = more if size is None else size + more
        y = pos_ref[0]
        source = lax.rem(y + by, NY)
        beside = y + 1 - 2 * lax.rem(y, 2)
        role = jnp.where(
            source == y, 0, jnp.where(source == 3 - y, 1, jnp.where(source == beside, 2, 3))
        )
        for out_ref, wanted in ((keep_ref, role < 2), (give_ref, role >= 2)):

            @pl.when(wanted)
            def _(out_ref=out_ref, score=score, size=size, place=lax.rem(role, 2)):
                out_ref[place, 0:1, :] = score
                out_ref[place, 1:2, :] = size


def local_scores(pos, own, others, here, there):
    points = own.shape[0] - 16
    vmem = pl.BlockSpec(memory_space=pltpu.VMEM)
    return pl.pallas_call(
        score_kernel,
        out_shape=(jax.ShapeDtypeStruct((2, 2, points), jnp.float32),) * 2
        + (jax.ShapeDtypeStruct((1, points), jnp.float32),),
        in_specs=[pl.BlockSpec(memory_space=pltpu.SMEM)] + [vmem] * 6,
        out_specs=(vmem,) * 3,
        compiler_params=LIMIT,
        name="local_scores",
    )(pos, *map(near, (own, *others, here, there)))


def steps(embeddings, assignment, slot_of, old_centroids):
    points = embeddings.shape[0]
    width = D // NC
    c = lax.axis_index("c")
    y = lax.axis_index("y")
    zl = lax.axis_index("zl")

    pos = jnp.stack([y, zl, c]).astype(jnp.int32)
    packed = pack(pos, assignment, slot_of, embeddings)
    far = shifted(packed, "y", NY, 2)
    after = shifted(packed, "y", NY, -1)
    before = shifted(packed, "y", NY, 1)
    others = [after, far, before]
    cent = exchange(old_centroids.reshape(3, NC, width).swapaxes(0, 1), "c")

    here = exchange(copies(cent.reshape(NC * 3, width), ZH), "zh", turned(ROW_TURN))
    here = here.reshape(ZH * NC * 3, width)

    away = local_sums(pos, packed, others, 2, True)
    beside = [(z, (z - 1 if z % ZL == 0 else z + 1) % NZ) for z in range(NZ)]
    arrived = shifted(away[0], "zl", ZL, 1), lax.ppermute(away[1], ("zh", "zl"), beside)
    (home,) = local_sums(pos, packed, others, 1, False)
    there = lax.ppermute(here, ("zh", "zl"), beside)
    both = merged(home, *arrived).reshape(ZH, NC * 3, width)
    summed = exchange(both, "zh", turned(SUM_TURN))
    summed = summed.sum(axis=0)

    keep, give, size = local_scores(pos, packed, others, here, there)
    kept = keep + lax.ppermute(give, "y", [(0, 1), (1, 0), (2, 3), (3, 2)])
    scored = kept[0] + lax.ppermute(kept[1], "y", [(0, 3), (3, 0), (1, 2), (2, 1)])

    sends = jnp.concatenate(
        [
            summed.reshape(NC, 1, 3 * width),
            jnp.broadcast_to(scored.reshape(1, 1, 2 * points), (NC, 1, 2 * points)),
            jnp.broadcast_to(size[None], (NC, 1, points)),
        ],
        axis=2,
    )
    got = exchange(sends, "c", turned(WHOLE_TURN))[:, 0]
    updated, distance = ending(got, old_centroids, points)
    return (updated, distance[0])


def solution(mesh):
    split = Mesh(mesh.devices.reshape(ZH, ZL, NY, NC), ("zh", "zl", "y", "c"))
    return jax.shard_map(
        steps,
        mesh=split,
        in_specs=(P(DP, None), P(DP), P(), P(CLUS_DP, None)),
        out_specs=(P(CLUS_DP, None), P(DP)),
        check_vma=False,
    )
```

```python
import functools

import jax
import jax.numpy as jnp
from jax import lax
from jax.experimental import pallas as pl
from jax.experimental.pallas import tpu as pltpu
from jax.sharding import Mesh
from jax.sharding import PartitionSpec as P


D = 4096
ZH, ZL, NY, NC = 8, 2, 4, 8
NZ = ZH * ZL
DP = ("zh", "zl", "y")
CLUS_DP = ("c", "zh", "zl", "y")
EPS = 1e-06


def shifted(x, axis, size, by):
    return lax.ppermute(x, axis, [(i, (i + by) % size) for i in range(size)])


def exchange(x, axis, order=None):
    groups = None if order is None else [list(order)]
    return lax.all_to_all(x, axis, 0, 0, tiled=True, axis_index_groups=groups)


def copies(x, count):
    return jnp.broadcast_to(x, (count, *x.shape))


ROW_TURN = 4
SUM_TURN = 4
WHOLE_TURN = 4
FEATURE_TURN = 7


def turned(by):
    return [(i + by) % 8 for i in range(8)]


LIMIT = pltpu.CompilerParams(vmem_limit_bytes=12 * 1024 * 1024)


def near(x):
    return pltpu.with_memory_space_constraint(x, pltpu.VMEM)


def far(x):
    return pltpu.with_memory_space_constraint(x, pltpu.HBM)


def pack_kernel(pos_ref, ids_ref, table_ref, emb_ref, out_ref, rows_ref, in_ref, list_ref, sems):
    points, width = emb_ref.shape[0], out_ref.shape[1]
    start = pl.multiple_of(pos_ref[2] * width, width)
    copy = pltpu.make_async_copy(
        emb_ref.at[:, pl.ds(start, width)], out_ref.at[pl.ds(0, points), :], sems.at[0]
    )
    copy.start()
    small = [
        pltpu.make_async_copy(ids_ref, in_ref, sems.at[1]),
        pltpu.make_async_copy(table_ref, list_ref, sems.at[2]),
    ]
    for each in small:
        each.start()
    for each in small:
        each.wait()
    groups = table_ref.shape[0] // 128
    rows_ref[...] = jnp.zeros(rows_ref.shape, jnp.float32)
    for g in range(groups):
        slots = list_ref[g * 128 : (g + 1) * 128].reshape(1, 128)
        rows_ref[g : g + 1, :] = lax.shift_right_logical(slots, 6).astype(jnp.float32)
        rows_ref[16 + g : 17 + g, :] = (slots & 63).astype(jnp.float32)
    ids = in_ref[...]
    low = lax.broadcasted_iota(jnp.int32, (128, points), 0) == (ids & 127)
    got = jnp.dot(
        rows_ref[...].astype(jnp.bfloat16),
        low.astype(jnp.float32).astype(jnp.bfloat16),
        preferred_element_type=jnp.float32,
    )
    high = lax.broadcasted_iota(jnp.int32, (16, points), 0)
    chosen = high == lax.shift_right_logical(ids, 7)
    coarse = jnp.sum(jnp.where(chosen, got[:16], 0.0), axis=0, keepdims=True)
    fine = jnp.sum(jnp.where(chosen, got[16:], 0.0), axis=0, keepdims=True)
    tail = jnp.where(high == 0, coarse, jnp.where(high == 1, fine, 0.0))
    out_ref[points : points + 16, :] = tail.astype(jnp.bfloat16)
    copy.wait()


def pack(pos, assignment, slot_of, embeddings):
    points, width = embeddings.shape[0], D // NC
    vmem = pl.BlockSpec(memory_space=pltpu.VMEM)
    return pl.pallas_call(
        pack_kernel,
        out_shape=jax.ShapeDtypeStruct((points + 16, width), jnp.bfloat16),
        in_specs=[pl.BlockSpec(memory_space=pltpu.SMEM)]
        + [pl.BlockSpec(memory_space=pltpu.HBM)] * 3,
        out_specs=vmem,
        scratch_shapes=[
            pltpu.VMEM((32, 128), jnp.float32),
            pltpu.VMEM((1, points), jnp.int32),
            pltpu.VMEM(slot_of.shape, jnp.int32),
            pltpu.SemaphoreType.DMA((3,)),
        ],
        compiler_params=LIMIT,
        name="pack",
    )(pos, *map(far, (assignment[None, :], slot_of, embeddings)))


def ending_kernel(got_ref, old_ref, new_ref, dist_ref):
    width = D // NC
    points = dist_ref.shape[1]
    old = old_ref[...].astype(jnp.float32)
    for i in range(NC):
        c = (i + WHOLE_TURN) % NC
        for k in range(3):
            new_ref[k : k + 1, c * width : (c + 1) * width] = got_ref[
                i : i + 1, k * width : (k + 1) * width
            ]
    overall = new_ref[...] + old
    size = jnp.mean(overall * overall, axis=1, keepdims=True)
    new_ref[...] = overall * lax.rsqrt(size + EPS)
    scores = jnp.sum(got_ref[:, 3 * width :], axis=0, keepdims=True)
    cent_rms = jnp.sqrt(scores[:, points : 2 * points] / jnp.float32(D) + EPS)
    root_mean = jnp.sqrt(scores[:, 2 * points :] / jnp.float32(D) + EPS)
    dist_ref[...] = 1.0 - scores[:, :points] / (jnp.float32(D) * root_mean * cent_rms)


def ending(got, old, points):
    vmem = pl.BlockSpec(memory_space=pltpu.VMEM)
    return pl.pallas_call(
        ending_kernel,
        out_shape=(
            jax.ShapeDtypeStruct(old.shape, jnp.float32),
            jax.ShapeDtypeStruct((1, points), jnp.float32),
        ),
        in_specs=[vmem, vmem],
        out_specs=(vmem, vmem),
        compiler_params=LIMIT,
        name="ending",
    )(near(got), near(old))


def slot_column(rows, pos_ref, partner, turn, c_turn):
    r = lax.broadcasted_iota(jnp.int32, (rows, 1), 0)
    per_z = NC * 3
    zh = (r // per_z + turn) % ZH
    c = ((r % per_z) // 3 + c_turn) % NC
    half = 1 - pos_ref[1] if partner else pos_ref[1]
    first = (half * NY + pos_ref[0]) * 3
    return c * (NZ * NY * 3) + zh * (ZL * NY * 3) + r % 3 + first


def id_row(ref, points):
    tail = ref[points : points + 16, :].astype(jnp.float32)
    return (tail[0:1, :] * 64.0 + tail[1:2, :]).astype(jnp.int32)


def sums_kernel(partner, pos_ref, own_ref, a_ref, b_ref, c_ref, *out_refs):
    points = own_ref.shape[0] - 16
    wanted = slot_column(out_refs[0].shape[0], pos_ref, partner, SUM_TURN, WHOLE_TURN)
    total = None
    for ref in (own_ref, a_ref, b_ref, c_ref):
        hot = (wanted == id_row(ref, points)).astype(jnp.float32).astype(jnp.bfloat16)
        got = jnp.dot(hot, ref[0:points, :], preferred_element_type=jnp.float32)
        total = got if total is None else total + got
    width = out_refs[0].shape[1]
    for i, out_ref in enumerate(out_refs):
        out_ref[...] = total[:, i * width : (i + 1) * width]


def local_sums(pos, own, others, cuts, partner):
    rows = ZH * NC * 3
    width = own.shape[1] // cuts
    vmem = pl.BlockSpec(memory_space=pltpu.VMEM)
    return pl.pallas_call(
        functools.partial(sums_kernel, partner),
        out_shape=(jax.ShapeDtypeStruct((rows, width), jnp.float32),) * cuts,
        in_specs=[pl.BlockSpec(memory_space=pltpu.SMEM)] + [vmem] * 4,
        out_specs=(vmem,) * cuts,
        compiler_params=LIMIT,
        name="local_sums",
    )(pos, *map(near, (own, *others)))


def merge_kernel(home_ref, a_ref, b_ref, out_ref):
    width = a_ref.shape[1]
    out_ref[:, :width] = home_ref[:, :width] + a_ref[...]
    out_ref[:, width:] = home_ref[:, width:] + b_ref[...]


def merged(home, a, b):
    vmem = pl.BlockSpec(memory_space=pltpu.VMEM)
    return pl.pallas_call(
        merge_kernel,
        out_shape=jax.ShapeDtypeStruct(home.shape, jnp.float32),
        in_specs=[vmem] * 3,
        out_specs=vmem,
        compiler_params=LIMIT,
        name="merged",
    )(*map(near, (home, a, b)))


def score_kernel(pos_ref, own_ref, a_ref, b_ref, c_ref, here_ref, there_ref, keep_ref, give_ref, size_ref):
    points = own_ref.shape[0] - 16
    wide = own_ref[0:points, :].astype(jnp.float32)
    wide = wide * wide
    high = wide.astype(jnp.bfloat16)
    low = (wide - high.astype(jnp.float32)).astype(jnp.bfloat16)
    ones = jnp.ones((16, wide.shape[1]), jnp.bfloat16)
    across = (((1,), (1,)), ((), ()))
    sizes = [
        lax.dot_general(ones, part, across, preferred_element_type=jnp.float32)
        for part in (high, low)
    ]
    size_ref[...] = (sizes[0] + sizes[1])[0:1, :]
    parts = []
    for partner, ref in enumerate((here_ref, there_ref)):
        rows = ref[...]
        wide = rows.astype(jnp.float32)
        square = jnp.sum(wide * wide, axis=1, keepdims=True)
        parts.append((rows, square, slot_column(rows.shape[0], pos_ref, partner, ROW_TURN, FEATURE_TURN)))
    for by, ref in enumerate((own_ref, a_ref, b_ref, c_ref)):
        ids = id_row(ref, points)
        score = size = None
        for rows, square, wanted in parts:
            raw = lax.dot_general(
                rows,
                ref[0:points, :],
                (((1,), (1,)), ((), ())),
                preferred_element_type=jnp.float32,
            )
            hit = wanted == ids
            got = jnp.sum(jnp.where(hit, raw, 0.0), axis=0, keepdims=True)
            more = jnp.sum(jnp.where(hit, square, 0.0), axis=0, keepdims=True)
            score = got if score is None else score + got
            size = more if size is None else size + more
        y = pos_ref[0]
        source = lax.rem(y + by, NY)
        beside = y + 1 - 2 * lax.rem(y, 2)
        role = jnp.where(
            source == y, 0, jnp.where(source == 3 - y, 1, jnp.where(source == beside, 2, 3))
        )
        for out_ref, wanted in ((keep_ref, role < 2), (give_ref, role >= 2)):

            @pl.when(wanted)
            def _(out_ref=out_ref, score=score, size=size, place=lax.rem(role, 2)):
                out_ref[place, 0:1, :] = score
                out_ref[place, 1:2, :] = size


def local_scores(pos, own, others, here, there):
    points = own.shape[0] - 16
    vmem = pl.BlockSpec(memory_space=pltpu.VMEM)
    return pl.pallas_call(
        score_kernel,
        out_shape=(jax.ShapeDtypeStruct((2, 2, points), jnp.float32),) * 2
        + (jax.ShapeDtypeStruct((1, points), jnp.float32),),
        in_specs=[pl.BlockSpec(memory_space=pltpu.SMEM)] + [vmem] * 6,
        out_specs=(vmem,) * 3,
        compiler_params=LIMIT,
        name="local_scores",
    )(pos, *map(near, (own, *others, here, there)))


def steps(embeddings, assignment, slot_of, old_centroids):
    points = embeddings.shape[0]
    width = D // NC
    c = lax.axis_index("c")
    y = lax.axis_index("y")
    zl = lax.axis_index("zl")

    pos = jnp.stack([y, zl, c]).astype(jnp.int32)
    packed = pack(pos, assignment, slot_of, embeddings)
    far = shifted(packed, "y", NY, 2)
    after = shifted(packed, "y", NY, -1)
    before = shifted(packed, "y", NY, 1)
    others = [after, far, before]
    cent = jnp.roll(old_centroids, -FEATURE_TURN * width, axis=1)
    cent = cent.reshape(3, NC, width).swapaxes(0, 1)
    cent = exchange(cent, "c", turned(FEATURE_TURN))

    here = exchange(copies(cent.reshape(NC * 3, width), ZH), "zh", turned(ROW_TURN))
    here = here.reshape(ZH * NC * 3, width)

    away = local_sums(pos, packed, others, 2, True)
    beside = [(z, (z - 1 if z % ZL == 0 else z + 1) % NZ) for z in range(NZ)]
    arrived = shifted(away[0], "zl", ZL, 1), lax.ppermute(away[1], ("zh", "zl"), beside)
    (home,) = local_sums(pos, packed, others, 1, False)
    there = lax.ppermute(here, ("zh", "zl"), beside)
    both = merged(home, *arrived).reshape(ZH, NC * 3, width)
    summed = exchange(both, "zh", turned(SUM_TURN))
    summed = summed.sum(axis=0)

    keep, give, size = local_scores(pos, packed, others, here, there)
    kept = keep + lax.ppermute(give, "y", [(0, 1), (1, 0), (2, 3), (3, 2)])
    scored = kept[0] + lax.ppermute(kept[1], "y", [(0, 3), (3, 0), (1, 2), (2, 1)])

    sends = jnp.concatenate(
        [
            summed.reshape(NC, 1, 3 * width),
            jnp.broadcast_to(scored.reshape(1, 1, 2 * points), (NC, 1, 2 * points)),
            jnp.broadcast_to(size[None], (NC, 1, points)),
        ],
        axis=2,
    )
    got = exchange(sends, "c", turned(WHOLE_TURN))[:, 0]
    updated, distance = ending(got, old_centroids, points)
    return (updated, distance[0])


def solution(mesh):
    split = Mesh(mesh.devices.reshape(ZH, ZL, NY, NC), ("zh", "zl", "y", "c"))
    return jax.shard_map(
        steps,
        mesh=split,
        in_specs=(P(DP, None), P(DP), P(), P(CLUS_DP, None)),
        out_specs=(P(CLUS_DP, None), P(DP)),
        check_vma=False,
    )
```
